128 devices in a mesh: rows: 4 (over x_lo, core), hidden: 32 (over x_hi, z, y).
Axes of the slice: x: 4 (x_hi: 2, x_lo: 2; x = x_hi * 2 + x_lo), y: 4, z: 4, core: 2. Of those that a mesh axis runs over, the one named last changes fastest.
Arguments:
- resid_stream: bfloat16 [1024, 3584], P('rows'), may hold values from -6 to 6
- pre_gain: float32 [3584], replicated, may hold values from -0.5 to 0.5
- w_gate: bfloat16 [3584, 14336], P(None, 'hidden'), may hold values from -0.09375 to 0.09375
- w_up: bfloat16 [3584, 14336], P(None, 'hidden'), may hold values from -0.09375 to 0.09375
- w_down: bfloat16 [14336, 3584], P('hidden'), may hold values from -0.09375 to 0.09375
- w_enc: bfloat16 [3584, 32768], P(None, ('rows', 'hidden')), may hold values from -0.09375 to 0.09375
- b_enc: bfloat16 [32768], P(('rows', 'hidden')), may hold values from -3 to 3
- w_dec: bfloat16 [32768, 3584], P(('rows', 'hidden')), may hold values from -0.03125 to 0.03125
- b_dec: float32 [3584], replicated, may hold values from -3 to 3
Outputs:
- enc_grad: float32 [3584, 32768], P(None, ('rows', 'hidden'))
- dec_grad: float32 [32768, 3584], P(('rows', 'hidden'))
The draws below stay inside these ranges and needn't reach their ends.
All inputs are finite; a program needn't handle non-finite values.
Results may differ from the reference program's by a relative error of at most 0.0062.
Values may be sent and summed in bfloat16 or wider, within the bound.
No kernel may reach another device: no remote copies, remote signals or barrier semaphores. Data moves between devices by JAX's collectives and lax.ppermute only.
A program may use at most 128 MiB of HBM per device.

```python
import jax
import jax.numpy as jnp
from jax import lax

D = 3584
FF = 14336
TOKENS = 1024
LAT = 32768


def strengthened(values, stream_key, source, target, shards_of, factor):
    def block_of(axis_at):
        return (jnp.arange(values.shape[axis_at]) // (values.shape[axis_at] // shards_of)).reshape((-1,) + (1,) * (values.ndim - 1 - axis_at))

    near = jax.random.permutation(stream_key, shards_of)[block_of(target)]
    far = (block_of(target) + shards_of // 2) % shards_of
    return jnp.where((block_of(source) == near) | (block_of(source) == far), factor * values, values)


def shard_levels(stream_key, shape, pieces, least, largest):
    level = 1.0
    for position, shards_of in pieces:
        heights = jax.random.uniform(jax.random.fold_in(jax.random.fold_in(stream_key, 6), position), (shards_of,), jnp.float32, least / len(pieces), largest / len(pieces))
        level = level * jnp.repeat(jnp.exp(heights), shape[position] // shards_of).reshape((-1,) + (1,) * (len(shape) - 1 - position))
    return level


def bell_draw(key, dims, width, limit, shards=(), kind=jnp.bfloat16):
    gain = shard_levels(key, dims, shards, -0.22, 0.18) if shards else 1.0
    array = jax.random.normal(key, dims, jnp.float32) * width * gain
    return jnp.minimum(jnp.maximum(array, -limit), limit).astype(kind)


def noise_with(rng, extent, deviation, most, pieces, heavy, kind=jnp.bfloat16):
    drawn = deviation * jax.random.normal(rng, extent, jnp.float32)
    if pieces:
        drawn = drawn * shard_levels(rng, extent, pieces, -0.22, 0.18)
    return jnp.clip(strengthened(drawn, jax.random.fold_in(rng, 3), *heavy), -most, most).astype(kind)


def setup_inputs(seed: int = 0) -> dict:
    seeds = jax.random.split(jax.random.key(seed), 10)
    return {
        "resid_stream": bell_draw(seeds[0], (TOKENS, D), 1.0, 6.0, ((0, 4),)),
        "pre_gain": jnp.clip(jax.random.uniform(seeds[1], (D,), jnp.float32, -0.5, 0.5), -0.5, 0.5),
        "w_gate": bell_draw(seeds[2], (D, FF), D ** -0.5, 0.09375, ((1, 32),)),
        "w_up": bell_draw(seeds[3], (D, FF), D ** -0.5, 0.09375, ((1, 32),)),
        "w_down": noise_with(seeds[4], (FF, D), FF ** -0.5, 0.09375, ((0, 32),), (0, 1, 32, 2.75)),
        "w_enc": bell_draw(seeds[5], (D, LAT), D ** -0.5, 0.09375, ((1, 128),)),
        "b_enc": bell_draw(seeds[6], (LAT,), 0.5, 3.0, ((0, 128),)),
        "w_dec": bell_draw(seeds[7], (LAT, D), LAT ** -0.5, 0.03125, ((0, 128),)),
        "b_dec": bell_draw(seeds[8], (D,), 0.5, 3.0, (), jnp.float32),
    }


def reference(resid_stream, pre_gain, w_gate, w_up, w_down, w_enc, b_enc, w_dec, b_dec):
    values = resid_stream.astype(jnp.float32)
    variance = lax.optimization_barrier(jnp.mean(values * values, axis=-1, keepdims=True))
    normal_in = (values * lax.rsqrt(variance + 1e-06) * (1.0 + pre_gain)).astype(jnp.bfloat16)
    gate_proj = jnp.dot(normal_in, w_gate, preferred_element_type=jnp.float32)
    up_proj = jnp.dot(normal_in, w_up, preferred_element_type=jnp.float32)
    hidden_units = (jax.nn.gelu(gate_proj, approximate=True) * up_proj).astype(jnp.bfloat16)
    target = jnp.dot(hidden_units, w_down, preferred_element_type=jnp.float32)
    pre_act = jnp.dot(normal_in, w_enc, preferred_element_type=jnp.float32) + b_enc.astype(jnp.float32)
    rectified = jnp.maximum(pre_act, 0.0)
    latent = (rectified * rectified).astype(jnp.bfloat16)
    recon = jnp.dot(latent, w_dec, preferred_element_type=jnp.float32) + b_dec
    misfit = (recon - target).astype(jnp.bfloat16)
    factor = 1.0 / TOKENS ** 0.5
    dec_grad = lax.dot_general(latent, misfit, (((0,), (0,)), ((), ())), preferred_element_type=jnp.float32) * factor
    back_prop = lax.dot_general(misfit, w_dec, (((1,), (1,)), ((), ())), preferred_element_type=jnp.float32)
    slope = (back_prop * 2.0 * rectified).astype(jnp.bfloat16)
    enc_grad = lax.dot_general(normal_in, slope, (((0,), (0,)), ((), ())), preferred_element_type=jnp.float32) * factor
    return (enc_grad, dec_grad)
```

```python
import math

import jax
import jax.numpy as jnp
from jax import lax
from jax.sharding import Mesh
from jax.sharding import PartitionSpec as P


F32 = jnp.float32
BF16 = jnp.bfloat16
ROWS = ("xl", "c")
HIDDEN = ("xh", "z", "y")
CHIPS = ("xl", "xh", "z", "y")


def normed(resid_stream, pre_gain):
    values = resid_stream.astype(F32)
    variance = jnp.mean(values * values, axis=-1, keepdims=True)
    return (values * lax.rsqrt(variance + 1e-06) * (1.0 + pre_gain)).astype(BF16)


def dot(left, right):
    return jnp.dot(left, right, preferred_element_type=F32)


def contract_first(left, right):
    return lax.dot_general(left, right, (((0,), (0,)), ((), ())), preferred_element_type=F32)


def contract_last(left, right):
    return lax.dot_general(left, right, (((1,), (1,)), ((), ())), preferred_element_type=F32)


def along_x(values, step):
    def index(x):
        return (x % 2) * 2 + x // 2

    return lax.ppermute(values, ("xl", "xh"), [(index(x), index((x + step) % 4)) for x in range(4)])


def other_core(values):
    return lax.ppermute(values, "c", [(0, 1), (1, 0)])


def swap_if(flag, values):
    half = values.shape[0] // 2
    return jnp.where(flag, jnp.concatenate([values[half:], values[:half]], axis=0), values)


def on_device(resid_stream, pre_gain, w_gate, w_up, w_down, w_enc, b_enc, w_dec, b_dec):
    rows, width = resid_stream.shape
    half = rows // 2
    factor = 1.0 / math.sqrt(rows * lax.axis_size(ROWS))
    odd = lax.axis_index("xl") == 1
    chips = lax.axis_size(CHIPS)

    far_resid = jnp.concatenate(
        [along_x(resid_stream[:half], 1), along_x(resid_stream[half:], -1)], axis=0
    )
    enc_2 = jnp.concatenate([w_enc, other_core(w_enc)], axis=1)
    dec_2 = jnp.concatenate([w_dec, other_core(w_dec)], axis=0)
    bias_2 = jnp.concatenate([b_enc, other_core(b_enc)], axis=0).astype(F32)

    near = normed(resid_stream, pre_gain)
    hidden_units = (jax.nn.gelu(dot(near, w_gate), approximate=True) * dot(near, w_up)).astype(BF16)
    far_resid, hidden_units = lax.optimization_barrier((far_resid, hidden_units))
    normal_in = jnp.concatenate([near, normed(far_resid, pre_gain)], axis=0)
    rectified = swap_if(odd, jnp.maximum(dot(normal_in, enc_2) + bias_2, 0.0))
    latent = (rectified * rectified).astype(BF16)
    mine = swap_if(odd, jnp.concatenate([hidden_units, jnp.zeros_like(hidden_units)], axis=0))
    part = (dot(latent, dec_2) - dot(mine, w_down)).astype(BF16)

    blocks = part.reshape(chips, part.shape[0] // chips, width)
    arrived = lax.all_to_all(blocks, CHIPS, 0, 0, tiled=True)
    misfit = (jnp.sum(arrived.astype(F32), axis=0) + b_dec).astype(BF16)
    spread = jnp.broadcast_to(misfit[None], (chips,) + misfit.shape)
    misfit_all = lax.all_to_all(spread, CHIPS, 0, 0, tiled=True).reshape(part.shape)

    mine_of = w_dec.shape[0]
    dec_part = contract_first(latent, misfit_all)
    dec_sum = dec_part[:mine_of] + other_core(dec_part[mine_of:].astype(BF16)).astype(F32)
    slope = (contract_last(misfit_all, dec_2) * 2.0 * rectified).astype(BF16)
    slope = swap_if(odd, slope)
    enc_part = contract_first(normal_in, slope)
    enc_sum = enc_part[:, :mine_of] + other_core(enc_part[:, mine_of:].astype(BF16)).astype(F32)
    return enc_sum * factor, dec_sum * factor


def solution(mesh):
    fine = Mesh(mesh.devices.reshape(2, 2, 2, 4, 4), ("xl", "c", "xh", "z", "y"))
    return jax.shard_map(
        on_device,
        mesh=fine,
        in_specs=(
            P(ROWS, None),
            P(),
            P(None, HIDDEN),
            P(None, HIDDEN),
            P(HIDDEN, None),
            P(None, ROWS + HIDDEN),
            P(ROWS + HIDDEN),
            P(ROWS + HIDDEN, None),
            P(),
        ),
        out_specs=(P(None, ROWS + HIDDEN), P(ROWS + HIDDEN, None)),
        check_vma=False,
    )
```

```python
import math

import jax
import jax.numpy as jnp
from jax import lax
from jax.sharding import Mesh
from jax.sharding import PartitionSpec as P


F32 = jnp.float32
BF16 = jnp.bfloat16
ROWS = ("xl", "c")
HIDDEN = ("xh", "z", "y")
ALL = ("xl", "c", "xh", "z", "y")


def normed(resid_stream, pre_gain):
    values = resid_stream.astype(F32)
    variance = jnp.mean(values * values, axis=-1, keepdims=True)
    return (values * lax.rsqrt(variance + 1e-06) * (1.0 + pre_gain)).astype(BF16)


def dot(left, right):
    return jnp.dot(left, right, preferred_element_type=F32)


def contract_first(left, right):
    return lax.dot_general(left, right, (((0,), (0,)), ((), ())), preferred_element_type=F32)


def contract_last(left, right):
    return lax.dot_general(left, right, (((1,), (1,)), ((), ())), preferred_element_type=F32)


def index_of(x, core, z, y):
    return (((x % 2) * 2 + core) * 2 + x // 2) * 16 + z * 4 + y


def devices():
    return [(x, core, z, y) for x in range(4) for core in range(2) for z in range(4) for y in range(4)]


def far_rows(values):
    pairs = [
        (index_of(x, core, z, y), index_of((x + 1 - 2 * core) % 4, core, z, y))
        for x, core, z, y in devices()
    ]
    return lax.ppermute(values, ALL, pairs)


def cube_groups(outer):
    groups = {}
    for x, core, z, y in devices():
        moved = [(v + core) % 4 for v in (x, z, y)]
        cube = tuple(v // 2 for v in moved)
        place = tuple(min(v, 3 - v) for v in moved)
        key, order = (cube, place) if outer else (place, cube)
        groups.setdefault((core, key), []).append((order, index_of(x, core, z, y)))
    return [[device for _, device in sorted(members)] for _, members in sorted(groups.items())]


def exchange(values, outer):
    return lax.all_to_all(values, ALL, 0, 0, axis_index_groups=cube_groups(outer), tiled=True)


def other_core(values):
    return lax.ppermute(values, "c", [(0, 1), (1, 0)])


def swap_if(flag, values):
    half = values.shape[0] // 2
    return jnp.where(flag, jnp.concatenate([values[half:], values[:half]], axis=0), values)


def on_device(resid_stream, pre_gain, w_gate, w_up, w_down, w_enc, b_enc, w_dec, b_dec):
    rows, width = resid_stream.shape
    factor = 1.0 / math.sqrt(rows * lax.axis_size(ROWS))
    odd = lax.axis_index("xl") == 1

    far_resid = far_rows(resid_stream)
    enc_2 = jnp.concatenate([w_enc, other_core(w_enc)], axis=1)
    dec_2 = jnp.concatenate([w_dec, other_core(w_dec)], axis=0)
    bias_2 = jnp.concatenate([b_enc, other_core(b_enc)], axis=0).astype(F32)

    near = normed(resid_stream, pre_gain)
    hidden_units = (jax.nn.gelu(dot(near, w_gate), approximate=True) * dot(near, w_up)).astype(BF16)
    far_resid, hidden_units = lax.optimization_barrier((far_resid, hidden_units))
    normal_in = jnp.concatenate([near, normed(far_resid, pre_gain)], axis=0)
    rectified = swap_if(odd, jnp.maximum(dot(normal_in, enc_2) + bias_2, 0.0))
    latent = (rectified * rectified).astype(BF16)
    mine = swap_if(odd, jnp.concatenate([hidden_units, jnp.zeros_like(hidden_units)], axis=0))
    part = (dot(latent, dec_2) - dot(mine, w_down)).astype(BF16)

    arrived = exchange(part.reshape(8, part.shape[0] // 8, width), True)
    summed = jnp.sum(arrived.astype(F32), axis=0).astype(BF16)
    arrived = exchange(summed.reshape(8, summed.shape[0] // 8, width), False)
    misfit = (jnp.sum(arrived.astype(F32), axis=0) + b_dec).astype(BF16)
    for outer in (False, True):
        spread = jnp.broadcast_to(misfit[None], (8,) + misfit.shape)
        misfit = exchange(spread, outer).reshape(8 * misfit.shape[0], width)
    misfit_all = misfit

    mine_of = w_dec.shape[0]
    dec_part = contract_first(latent, misfit_all)
    dec_sum = dec_part[:mine_of] + other_core(dec_part[mine_of:].astype(BF16)).astype(F32)
    slope = (contract_last(misfit_all, dec_2) * 2.0 * rectified).astype(BF16)
    slope = swap_if(odd, slope)
    enc_part = contract_first(normal_in, slope)
    enc_sum = enc_part[:, :mine_of] + other_core(enc_part[:, mine_of:].astype(BF16)).astype(F32)
    return enc_sum * factor, dec_sum * factor


def solution(mesh):
    fine = Mesh(mesh.devices.reshape(2, 2, 2, 4, 4), ("xl", "c", "xh", "z", "y"))
    return jax.shard_map(
        on_device,
        mesh=fine,
        in_specs=(
            P(ROWS, None),
            P(),
            P(None, HIDDEN),
            P(None, HIDDEN),
            P(HIDDEN, None),
            P(None, ROWS + HIDDEN),
            P(ROWS + HIDDEN),
            P(ROWS + HIDDEN, None),
            P(),
        ),
        out_specs=(P(None, ROWS + HIDDEN), P(ROWS + HIDDEN, None)),
        check_vma=False,
    )
```

```python
import math

import jax
import jax.numpy as jnp
from jax import lax
from jax.experimental import pallas as pl
from jax.sharding import Mesh
from jax.sharding import PartitionSpec as P


F32 = jnp.float32
BF16 = jnp.bfloat16
ROWS = ("xl", "c")
HIDDEN = ("xh", "z", "y")
ALL = ("xl", "c", "xh", "z", "y")


def norm_kernel(values_ref, gain_ref, out_ref):
    values = values_ref[...].astype(F32)
    variance = jnp.mean(values * values, axis=-1, keepdims=True)
    out_ref[...] = (values * lax.rsqrt(variance + 1e-06) * (1.0 + gain_ref[...])).astype(BF16)


def normed(resid_stream, pre_gain):
    rows, width = resid_stream.shape
    step = 64
    return pl.pallas_call(
        norm_kernel,
        grid=(rows // step,),
        in_specs=[
            pl.BlockSpec((step, width), lambda i: (i, 0)),
            pl.BlockSpec((1, width), lambda i: (0, 0)),
        ],
        out_specs=pl.BlockSpec((step, width), lambda i: (i, 0)),
        out_shape=jax.ShapeDtypeStruct((rows, width), BF16),
        name="norm",
    )(resid_stream, pre_gain.reshape(1, width))


def dot(left, right):
    return jnp.dot(left, right, preferred_element_type=F32)


def contract_first(left, right):
    return lax.dot_general(left, right, (((0,), (0,)), ((), ())), preferred_element_type=F32)


def contract_last(left, right):
    return lax.dot_general(left, right, (((1,), (1,)), ((), ())), preferred_element_type=F32)


def index_of(x, core, z, y):
    return (((x % 2) * 2 + core) * 2 + x // 2) * 16 + z * 4 + y


def devices():
    return [(x, core, z, y) for x in range(4) for core in range(2) for z in range(4) for y in range(4)]


def far_rows(values):
    pairs = [
        (index_of(x, core, z, y), index_of((x + 1 - 2 * core) % 4, core, z, y))
        for x, core, z, y in devices()
    ]
    return lax.ppermute(values, ALL, pairs)


def cube_groups(outer):
    groups = {}
    for x, core, z, y in devices():
        moved = [(v + core) % 4 for v in (x, z, y)]
        cube = tuple(v // 2 for v in moved)
        place = tuple(min(v, 3 - v) for v in moved)
        key, order = (cube, place) if outer else (place, cube)
        groups.setdefault((core, key), []).append((order, index_of(x, core, z, y)))
    return [[device for _, device in sorted(members)] for _, members in sorted(groups.items())]


def exchange(values, outer):
    return lax.all_to_all(values, ALL, 0, 0, axis_index_groups=cube_groups(outer), tiled=True)


def other_core(values):
    return lax.ppermute(values, "c", [(0, 1), (1, 0)])


def swap_if(flag, values):
    half = values.shape[0] // 2
    return jnp.where(flag, jnp.concatenate([values[half:], values[:half]], axis=0), values)


def on_device(resid_stream, pre_gain, w_gate, w_up, w_down, w_enc, b_enc, w_dec, b_dec):
    rows, width = resid_stream.shape
    factor = 1.0 / math.sqrt(rows * lax.axis_size(ROWS))
    odd = lax.axis_index("xl") == 1

    far_resid = far_rows(resid_stream)
    enc_2 = jnp.concatenate([w_enc, other_core(w_enc)], axis=1)
    dec_2 = jnp.concatenate([w_dec, other_core(w_dec)], axis=0)
    bias_2 = jnp.concatenate([b_enc, other_core(b_enc)], axis=0).astype(F32)

    near = normed(resid_stream, pre_gain)
    hidden_units = (jax.nn.gelu(dot(near, w_gate), approximate=True) * dot(near, w_up)).astype(BF16)
    mine = swap_if(odd, jnp.concatenate([hidden_units, jnp.zeros_like(hidden_units)], axis=0))
    target = dot(mine, w_down)
    near_act = jnp.maximum(dot(near, enc_2) + bias_2, 0.0)
    far_resid, target, near_act, enc_2, dec_2 = lax.optimization_barrier(
        (far_resid, target, near_act, enc_2, dec_2)
    )
    far = normed(far_resid, pre_gain)
    far_act = jnp.maximum(dot(far, enc_2) + bias_2, 0.0)
    rectified = swap_if(odd, jnp.concatenate([near_act, far_act], axis=0))
    latent = (rectified * rectified).astype(BF16)
    part = (dot(latent, dec_2) - target).astype(BF16)

    arrived = exchange(part.reshape(8, part.shape[0] // 8, width), True)
    summed = jnp.sum(arrived.astype(F32), axis=0).astype(BF16)
    arrived = exchange(summed.reshape(8, summed.shape[0] // 8, width), False)
    misfit = (jnp.sum(arrived.astype(F32), axis=0) + b_dec).astype(BF16)
    for outer in (False, True):
        spread = jnp.broadcast_to(misfit[None], (8,) + misfit.shape)
        misfit = exchange(spread, outer).reshape(8 * misfit.shape[0], width)
    misfit_all = misfit

    own = w_dec.shape[0]
    dec_sent = other_core(contract_first(latent[:, own:], misfit_all).astype(BF16))
    slope = (contract_last(misfit_all, dec_2) * 2.0 * rectified).astype(BF16)
    slope = swap_if(odd, slope)
    normal_in = jnp.concatenate([near, far], axis=0)
    enc_out = contract_first(normal_in, slope[:, own:]).astype(BF16)
    enc_sent = other_core(enc_out)
    latent, slope, enc_out = lax.optimization_barrier((latent, slope, enc_out))
    dec_sum = contract_first(latent[:, :own], misfit_all) + dec_sent.astype(F32)
    enc_sum = contract_first(normal_in, slope[:, :own]) + enc_sent.astype(F32)
    return enc_sum * factor, dec_sum * factor


def solution(mesh):
    fine = Mesh(mesh.devices.reshape(2, 2, 2, 4, 4), ("xl", "c", "xh", "z", "y"))
    return jax.shard_map(
        on_device,
        mesh=fine,
        in_specs=(
            P(ROWS, None),
            P(),
            P(None, HIDDEN),
            P(None, HIDDEN),
            P(HIDDEN, None),
            P(None, ROWS + HIDDEN),
            P(ROWS + HIDDEN),
            P(ROWS + HIDDEN, None),
            P(),
        ),
        out_specs=(P(None, ROWS + HIDDEN), P(ROWS + HIDDEN, None)),
        check_vma=False,
    )
```

```python
import math

import jax
import jax.numpy as jnp
from jax import lax
from jax.sharding import Mesh
from jax.sharding import PartitionSpec as P


F32 = jnp.float32
BF16 = jnp.bfloat16
ROWS = ("xl", "c")
HIDDEN = ("xh", "z", "y")
ALL = ("xl", "c", "xh", "z", "y")
SHIFTS = ((0, 0, 1), (1, 1, 0))


def scale_of(values):
    values = values.astype(F32)
    return lax.rsqrt(jnp.mean(values * values, axis=-1, keepdims=True) + 1e-06)


def normed(values, scale, pre_gain):
    return (values.astype(F32) * scale * (1.0 + pre_gain)).astype(BF16)


def dot(left, right):
    return jnp.dot(left, right, preferred_element_type=F32)


def contract_first(left, right):
    return lax.dot_general(left, right, (((0,), (0,)), ((), ())), preferred_element_type=F32)


def contract_last(left, right):
    return lax.dot_general(left, right, (((1,), (1,)), ((), ())), preferred_element_type=F32)


def index_of(x, core, z, y):
    return (((x % 2) * 2 + core) * 2 + x // 2) * 16 + z * 4 + y


def devices():
    return [(x, core, z, y) for x in range(4) for core in range(2) for z in range(4) for y in range(4)]


def far_rows(values):
    pairs = [
        (index_of(x, core, z, y), index_of((x + 1 - 2 * core) % 4, core, z, y))
        for x, core, z, y in devices()
    ]
    return lax.ppermute(values, ALL, pairs)


def cube_groups(outer):
    groups = {}
    for x, core, z, y in devices():
        moved = [(v + step) % 4 for v, step in zip((x, z, y), SHIFTS[core])]
        cube = tuple(v // 2 for v in moved)
        place = tuple(min(v, 3 - v) for v in moved)
        key, order = (cube, place) if outer else (place, cube)
        groups.setdefault((core, key), []).append((order, index_of(x, core, z, y)))
    return [[device for _, device in sorted(members)] for _, members in sorted(groups.items())]


def exchange(values, outer):
    return lax.all_to_all(values, ALL, 0, 0, axis_index_groups=cube_groups(outer), tiled=True)


def other_core(values):
    return lax.ppermute(values, "c", [(0, 1), (1, 0)])


def swap_if(flag, values):
    half = values.shape[0] // 2
    return jnp.where(flag, jnp.concatenate([values[half:], values[:half]], axis=0), values)


def on_device(resid_stream, pre_gain, w_gate, w_up, w_down, w_enc, b_enc, w_dec, b_dec):
    rows, width = resid_stream.shape
    factor = 1.0 / math.sqrt(rows * lax.axis_size(ROWS))
    odd = lax.axis_index("xl") == 1

    far_resid = far_rows(resid_stream)
    enc_2 = jnp.concatenate([w_enc, other_core(w_enc)], axis=1)
    dec_2 = jnp.concatenate([w_dec, other_core(w_dec)], axis=0)
    bias_2 = jnp.concatenate([b_enc, other_core(b_enc)], axis=0).astype(F32)

    scale = scale_of(resid_stream)
    far_scale = far_rows(scale)
    near = normed(resid_stream, scale, pre_gain)
    hidden_units = (jax.nn.gelu(dot(near, w_gate), approximate=True) * dot(near, w_up)).astype(BF16)
    mine = swap_if(odd, jnp.concatenate([hidden_units, jnp.zeros_like(hidden_units)], axis=0))
    target = dot(mine, w_down)
    near_act = jnp.maximum(dot(near, enc_2) + bias_2, 0.0)
    far_resid, target, near_act, dec_2 = lax.optimization_barrier((far_resid, target, near_act, dec_2))
    far = normed(far_resid, far_scale, pre_gain)
    far_act = jnp.maximum(dot(far, enc_2) + bias_2, 0.0)
    rectified = swap_if(odd, jnp.concatenate([near_act, far_act], axis=0))
    latent = (rectified * rectified).astype(BF16)
    part = (dot(latent, dec_2) - target).astype(BF16)

    arrived = exchange(part.reshape(8, part.shape[0] // 8, width), True)
    summed = jnp.sum(arrived.astype(F32), axis=0).astype(BF16)
    arrived = exchange(summed.reshape(8, summed.shape[0] // 8, width), False)
    misfit = (jnp.sum(arrived.astype(F32), axis=0) + b_dec).astype(BF16)
    for outer in (False, True):
        spread = jnp.broadcast_to(misfit[None], (8,) + misfit.shape)
        misfit = exchange(spread, outer).reshape(8 * misfit.shape[0], width)
    misfit_all = misfit

    own = w_dec.shape[0]
    dec_out = contract_first(latent[:, own:], misfit_all).astype(BF16)
    dec_sent = other_core(dec_out)
    misfit_all, dec_out = lax.optimization_barrier((misfit_all, dec_out))
    slope = (contract_last(misfit_all, dec_2) * 2.0 * rectified).astype(BF16)
    slope = swap_if(odd, slope)
    normal_in = jnp.concatenate([near, far], axis=0)
    enc_out = contract_first(normal_in, slope[:, own:]).astype(BF16)
    enc_sent = other_core(enc_out)
    latent, slope, enc_out = lax.optimization_barrier((latent, slope, enc_out))
    dec_sum = contract_first(latent[:, :own], misfit_all) + dec_sent.astype(F32)
    enc_sum = contract_first(normal_in, slope[:, :own]) + enc_sent.astype(F32)
    return enc_sum * factor, dec_sum * factor


def solution(mesh):
    fine = Mesh(mesh.devices.reshape(2, 2, 2, 4, 4), ("xl", "c", "xh", "z", "y"))
    return jax.shard_map(
        on_device,
        mesh=fine,
        in_specs=(
            P(ROWS, None),
            P(),
            P(None, HIDDEN),
            P(None, HIDDEN),
            P(HIDDEN, None),
            P(None, ROWS + HIDDEN),
            P(ROWS + HIDDEN),
            P(ROWS + HIDDEN, None),
            P(),
        ),
        out_specs=(P(None, ROWS + HIDDEN), P(ROWS + HIDDEN, None)),
        check_vma=False,
    )
```

```python
import math

import jax
import jax.numpy as jnp
from jax import lax
from jax.sharding import Mesh
from jax.sharding import PartitionSpec as P


F32 = jnp.float32
BF16 = jnp.bfloat16
ROWS = ("xl", "c")
HIDDEN = ("xh", "z", "y")
ALL = ("xl", "c", "xh", "z", "y")
SHIFTS = ((0, 0, 1), (1, 1, 0))


def scale_of(values):
    values = values.astype(F32)
    return lax.rsqrt(jnp.mean(values * values, axis=-1, keepdims=True) + 1e-06)


def normed(values, scale, gain):
    return (values.astype(F32) * scale * gain).astype(BF16)


def dot(left, right):
    return jnp.dot(left, right, preferred_element_type=F32)


def contract_first(left, right):
    return lax.dot_general(left, right, (((0,), (0,)), ((), ())), preferred_element_type=F32)


def contract_last(left, right):
    return lax.dot_general(left, right, (((1,), (1,)), ((), ())), preferred_element_type=F32)


def index_of(x, core, z, y):
    return (((x % 2) * 2 + core) * 2 + x // 2) * 16 + z * 4 + y


def devices():
    return [(x, core, z, y) for x in range(4) for core in range(2) for z in range(4) for y in range(4)]


def far_rows(values):
    pairs = [
        (index_of(x, core, z, y), index_of((x + 1 - 2 * core) % 4, core, z, y))
        for x, core, z, y in devices()
    ]
    return lax.ppermute(values, ALL, pairs)


def cube_groups(outer):
    groups = {}
    for x, core, z, y in devices():
        moved = [(v + step) % 4 for v, step in zip((x, z, y), SHIFTS[core])]
        cube = tuple(v // 2 for v in moved)
        place = tuple(min(v, 3 - v) for v in moved)
        key, order = (cube, place) if outer else (place, cube)
        groups.setdefault((core, key), []).append((order, index_of(x, core, z, y)))
    return [[device for _, device in sorted(members)] for _, members in sorted(groups.items())]


def exchange(values, outer):
    blocks = values.reshape(8, values.shape[0] // 8, values.shape[1])
    return lax.all_to_all(blocks, ALL, 0, 0, axis_index_groups=cube_groups(outer), tiled=True)


def spread(values, outer):
    copies = jnp.broadcast_to(values[None], (8,) + values.shape)
    got = lax.all_to_all(copies, ALL, 0, 0, axis_index_groups=cube_groups(outer), tiled=True)
    return got.reshape(8 * values.shape[0], values.shape[1])


def added(blocks):
    total = blocks[0].astype(F32)
    for block in blocks[1:]:
        total = total + block.astype(F32)
    return total


def other_core(values):
    return lax.ppermute(values, "c", [(0, 1), (1, 0)])


def paired(flag, first, second, blocks):
    rows, width = first.shape
    first, second = (v.reshape(blocks, 1, rows // blocks, width) for v in (first, second))
    forth = jnp.concatenate([first, second], axis=1)
    back = jnp.concatenate([second, first], axis=1)
    return jnp.where(flag, back, forth).reshape(2 * rows, width)


def on_device(resid_stream, pre_gain, w_gate, w_up, w_down, w_enc, b_enc, w_dec, b_dec):
    rows, _ = resid_stream.shape
    factor = 1.0 / math.sqrt(rows * lax.axis_size(ROWS))
    odd = lax.axis_index("xl") == 1

    far_resid = far_rows(resid_stream)
    enc_2 = jnp.concatenate([w_enc, other_core(w_enc)], axis=1)
    dec_2 = jnp.concatenate([w_dec, other_core(w_dec)], axis=0)
    bias_2 = jnp.concatenate([b_enc, other_core(b_enc)], axis=0).astype(F32)

    scale = scale_of(resid_stream)
    far_scale = far_rows(scale)
    near = normed(resid_stream, scale, 1.0 + pre_gain)
    hidden_units = (jax.nn.gelu(dot(near, w_gate), approximate=True) * dot(near, w_up)).astype(BF16)
    hidden_units = lax.optimization_barrier(hidden_units)
    near_act = jnp.maximum(dot(near, enc_2) + bias_2, 0.0)
    near_part = (
        dot((near_act * near_act).astype(BF16), dec_2) - dot(hidden_units, w_down)
    ).astype(BF16)
    far_resid, _ = lax.optimization_barrier((far_resid, near_part))
    got_near = exchange(near_part, True)
    gain = lax.optimization_barrier(pre_gain)
    gain = 1.0 + gain
    gain = lax.optimization_barrier(gain)
    far = normed(far_resid, far_scale, gain)
    far_act = jnp.maximum(dot(far, enc_2) + bias_2, 0.0)
    far_part = dot((far_act * far_act).astype(BF16), dec_2).astype(BF16)
    got_far = exchange(far_part, True)
    core = lax.axis_index("c")
    step = SHIFTS[0][0] + core * (SHIFTS[1][0] - SHIFTS[0][0])
    x = 2 * lax.axis_index("xh") + lax.axis_index("xl")
    turned = ((x + step) % 4 // 2 + step) % 2 == 1
    low = added(got_near[:4]) + added(got_far[4:])
    high = added(got_near[4:]) + added(got_far[:4])
    summed = paired(turned, low, high, 1).astype(BF16)
    misfit = (added(exchange(summed, False)) + b_dec).astype(BF16)
    misfit_all = spread(spread(misfit, False), True)

    rectified = paired(odd, near_act, far_act, 8)
    latent = (rectified * rectified).astype(BF16)

    own = w_dec.shape[0]
    dec_out = contract_first(latent[:, own:], misfit_all).astype(BF16)
    dec_sent = other_core(dec_out)
    misfit_all, dec_out = lax.optimization_barrier((misfit_all, dec_out))
    slope = (contract_last(misfit_all, dec_2) * 2.0 * rectified).astype(BF16)
    slope = slope.reshape(8, 2, -1, slope.shape[1])
    near_slope = jnp.where(odd, slope[:, 1], slope[:, 0]).reshape(rows, -1)
    far_slope = jnp.where(odd, slope[:, 0], slope[:, 1]).reshape(rows, -1)
    slope = jnp.concatenate([near_slope, far_slope], axis=0)
    normal_in = jnp.concatenate([near, far], axis=0)
    enc_out = contract_first(normal_in, slope[:, own:]).astype(BF16)
    enc_sent = other_core(enc_out)
    latent, slope, enc_out = lax.optimization_barrier((latent, slope, enc_out))
    dec_sum = (contract_first(latent[:, :own], misfit_all) + dec_sent.astype(F32)) * factor
    enc_sum = (contract_first(normal_in, slope[:, :own]) + enc_sent.astype(F32)) * factor
    return enc_sum, dec_sum


def solution(mesh):
    fine = Mesh(mesh.devices.reshape(2, 2, 2, 4, 4), ("xl", "c", "xh", "z", "y"))
    return jax.shard_map(
        on_device,
        mesh=fine,
        in_specs=(
            P(ROWS, None),
            P(),
            P(None, HIDDEN),
            P(None, HIDDEN),
            P(HIDDEN, None),
            P(None, ROWS + HIDDEN),
            P(ROWS + HIDDEN),
            P(ROWS + HIDDEN, None),
            P(),
        ),
        out_specs=(P(None, ROWS + HIDDEN), P(ROWS + HIDDEN, None)),
        check_vma=False,
    )
```

```python
import math

import jax
import jax.numpy as jnp
from jax import lax
from jax.sharding import Mesh
from jax.sharding import PartitionSpec as P


F32 = jnp.float32
BF16 = jnp.bfloat16
ROWS = ("xl", "c")
HIDDEN = ("xh", "z", "y")
ALL = ("xl", "c", "xh", "z", "y")
SHIFTS = ((1, 1, 0), (0, 0, 1))


def scale_of(values):
    values = values.astype(F32)
    return lax.rsqrt(jnp.mean(values * values, axis=-1, keepdims=True) + 1e-06)


def normed(values, scale, pre_gain):
    return (values.astype(F32) * scale * (1.0 + pre_gain)).astype(BF16)


def dot(left, right):
    return jnp.dot(left, right, preferred_element_type=F32)


def contract_first(left, right):
    return lax.dot_general(left, right, (((0,), (0,)), ((), ())), preferred_element_type=F32)


def contract_last(left, right):
    return lax.dot_general(left, right, (((1,), (1,)), ((), ())), preferred_element_type=F32)


def index_of(x, core, z, y):
    return (((x % 2) * 2 + core) * 2 + x // 2) * 16 + z * 4 + y


def devices():
    return [(x, core, z, y) for x in range(4) for core in range(2) for z in range(4) for y in range(4)]


def far_rows(values):
    pairs = [
        (index_of(x, core, z, y), index_of((x + 1 - 2 * core) % 4, core, z, y))
        for x, core, z, y in devices()
    ]
    return lax.ppermute(values, ALL, pairs)


def cube_groups(outer):
    groups = {}
    for x, core, z, y in devices():
        moved = [(v + step) % 4 for v, step in zip((x, z, y), SHIFTS[core])]
        cube = tuple(v // 2 for v in moved)
        place = tuple(min(v, 3 - v) for v in moved)
        key, order = (cube, place) if outer else (place, cube)
        groups.setdefault((core, key), []).append((order, index_of(x, core, z, y)))
    return [[device for _, device in sorted(members)] for _, members in sorted(groups.items())]


def exchange(values, outer):
    return lax.all_to_all(values, ALL, 0, 0, axis_index_groups=cube_groups(outer), tiled=True)


def other_core(values):
    return lax.ppermute(values, "c", [(0, 1), (1, 0)])


def added(blocks):
    total = blocks[0].astype(F32)
    for block in blocks[1:]:
        total = total + block.astype(F32)
    return total


def swap_if(flag, values):
    half = values.shape[0] // 2
    return jnp.where(flag, jnp.concatenate([values[half:], values[:half]], axis=0), values)


def on_device(resid_stream, pre_gain, w_gate, w_up, w_down, w_enc, b_enc, w_dec, b_dec):
    rows, width = resid_stream.shape
    factor = 1.0 / math.sqrt(rows * lax.axis_size(ROWS))
    odd = lax.axis_index("xl") == 1

    far_resid = far_rows(resid_stream)
    enc_2 = jnp.concatenate([w_enc, other_core(w_enc)], axis=1)
    dec_2 = jnp.concatenate([w_dec, other_core(w_dec)], axis=0)
    bias_2 = jnp.concatenate([b_enc, other_core(b_enc)], axis=0).astype(F32)

    scale = scale_of(resid_stream)
    far_scale = far_rows(scale)
    near = normed(resid_stream, scale, pre_gain)
    hidden_units = (jax.nn.gelu(dot(near, w_gate), approximate=True) * dot(near, w_up)).astype(BF16)
    mine = swap_if(odd, jnp.concatenate([hidden_units, jnp.zeros_like(hidden_units)], axis=0))
    target = dot(mine, w_down)
    near_act = jnp.maximum(dot(near, enc_2) + bias_2, 0.0)
    far_resid, target, near_act, dec_2 = lax.optimization_barrier((far_resid, target, near_act, dec_2))
    far = normed(far_resid, far_scale, pre_gain)
    far_act = jnp.maximum(dot(far, enc_2) + bias_2, 0.0)
    rectified = swap_if(odd, jnp.concatenate([near_act, far_act], axis=0))
    latent = (rectified * rectified).astype(BF16)
    part = (dot(latent, dec_2) - target).astype(BF16)

    arrived = exchange(part.reshape(8, part.shape[0] // 8, width), True)
    summed = added(arrived).astype(BF16)
    arrived = exchange(summed.reshape(8, summed.shape[0] // 8, width), False)
    misfit = (added(arrived) + b_dec).astype(BF16)
    for outer in (False, True):
        spread = jnp.broadcast_to(misfit[None], (8,) + misfit.shape)
        misfit = exchange(spread, outer).reshape(8 * misfit.shape[0], width)
    misfit_all = misfit

    own = w_dec.shape[0]
    dec_out = contract_first(latent[:, own:], misfit_all).astype(BF16)
    dec_sent = other_core(dec_out)
    misfit_all, dec_out = lax.optimization_barrier((misfit_all, dec_out))
    slope = (contract_last(misfit_all, dec_2) * 2.0 * rectified).astype(BF16)
    slope = swap_if(odd, slope)
    normal_in = jnp.concatenate([near, far], axis=0)
    enc_out = contract_first(normal_in, slope[:, own:]).astype(BF16)
    enc_sent = other_core(enc_out)
    latent, slope, enc_out = lax.optimization_barrier((latent, slope, enc_out))
    dec_sum = (contract_first(latent[:, :own], misfit_all) + dec_sent.astype(F32)) * factor
    enc_sum = (contract_first(normal_in, slope[:, :own]) + enc_sent.astype(F32)) * factor
    return enc_sum, dec_sum


def solution(mesh):
    fine = Mesh(mesh.devices.reshape(2, 2, 2, 4, 4), ("xl", "c", "xh", "z", "y"))
    return jax.shard_map(
        on_device,
        mesh=fine,
        in_specs=(
            P(ROWS, None),
            P(),
            P(None, HIDDEN),
            P(None, HIDDEN),
            P(HIDDEN, None),
            P(None, ROWS + HIDDEN),
            P(ROWS + HIDDEN),
            P(ROWS + HIDDEN, None),
            P(),
        ),
        out_specs=(P(None, ROWS + HIDDEN), P(ROWS + HIDDEN, None)),
        check_vma=False,
    )
```

```python
import math

import jax
import jax.numpy as jnp
from jax import lax
from jax.sharding import Mesh
from jax.sharding import PartitionSpec as P


F32 = jnp.float32
BF16 = jnp.bfloat16
ROWS = ("xl", "c")
HIDDEN = ("xh", "z", "y")
ALL = ("xl", "c", "xh", "z", "y")
LINE = 4


def scale_of(values):
    values = values.astype(F32)
    return lax.rsqrt(jnp.mean(values * values, axis=-1, keepdims=True) + 1e-06)


def normed(values, scale, gain):
    return (values.astype(F32) * scale * gain).astype(BF16)


def dot(left, right):
    return jnp.dot(left, right, preferred_element_type=F32)


def contract_first(left, right):
    return lax.dot_general(left, right, (((0,), (0,)), ((), ())), preferred_element_type=F32)


def contract_last(left, right):
    return lax.dot_general(left, right, (((1,), (1,)), ((), ())), preferred_element_type=F32)


def index_of(x, core, z, y):
    return (((x % 2) * 2 + core) * 2 + x // 2) * 16 + z * 4 + y


def devices():
    return [(x, core, z, y) for x in range(4) for core in range(2) for z in range(4) for y in range(4)]


def far_rows(values):
    pairs = [
        (index_of(x, core, z, y), index_of((x + 1 - 2 * core) % 4, core, z, y))
        for x, core, z, y in devices()
    ]
    return lax.ppermute(values, ALL, pairs)


def groups_of(line):
    groups = {}
    for x, core, z, y in devices():
        place, plane = ((y,), (x, z)) if core == 0 else ((z,), (x, y))
        key, order = (plane, place) if line else (place, plane)
        groups.setdefault((core, key), []).append((order, index_of(x, core, z, y)))
    return [[device for _, device in sorted(members)] for _, members in sorted(groups.items())]


def exchange(values, line):
    groups = groups_of(line)
    size = len(groups[0])
    blocks = values.reshape(size, values.shape[0] // size, values.shape[1])
    return lax.all_to_all(blocks, ALL, 0, 0, axis_index_groups=groups, tiled=True)


def spread(values, line):
    groups = groups_of(line)
    size = len(groups[0])
    copies = jnp.broadcast_to(values[None], (size,) + values.shape)
    got = lax.all_to_all(copies, ALL, 0, 0, axis_index_groups=groups, tiled=True)
    return got.reshape(size * values.shape[0], values.shape[1])


def added(blocks):
    total = blocks[0].astype(F32)
    for block in blocks[1:]:
        total = total + block.astype(F32)
    return total


def other_core(values):
    return lax.ppermute(values, "c", [(0, 1), (1, 0)])


def paired(flag, first, second, blocks):
    rows, width = first.shape
    first, second = (v.reshape(blocks, 1, rows // blocks, width) for v in (first, second))
    forth = jnp.concatenate([first, second], axis=1)
    back = jnp.concatenate([second, first], axis=1)
    return jnp.where(flag, back, forth).reshape(2 * rows, width)


def on_device(resid_stream, pre_gain, w_gate, w_up, w_down, w_enc, b_enc, w_dec, b_dec):
    rows, _ = resid_stream.shape
    factor = 1.0 / math.sqrt(rows * lax.axis_size(ROWS))
    odd = lax.axis_index("xl") == 1

    far_resid = far_rows(resid_stream)
    enc_2 = jnp.concatenate([w_enc, other_core(w_enc)], axis=1)
    dec_2 = jnp.concatenate([w_dec, other_core(w_dec)], axis=0)
    bias_2 = jnp.concatenate([b_enc, other_core(b_enc)], axis=0).astype(F32)

    scale = scale_of(resid_stream)
    far_scale = far_rows(scale)
    near = normed(resid_stream, scale, 1.0 + pre_gain)
    hidden_units = (jax.nn.gelu(dot(near, w_gate), approximate=True) * dot(near, w_up)).astype(BF16)
    hidden_units = lax.optimization_barrier(hidden_units)
    near_act = jnp.maximum(dot(near, enc_2) + bias_2, 0.0)
    near_part = (
        dot((near_act * near_act).astype(BF16), dec_2) - dot(hidden_units, w_down)
    ).astype(BF16)
    far_resid, _ = lax.optimization_barrier((far_resid, near_part))
    got_near = exchange(near_part, True)
    gain = lax.optimization_barrier(pre_gain)
    gain = 1.0 + gain
    gain = lax.optimization_barrier(gain)
    far = normed(far_resid, far_scale, gain)
    far_act = jnp.maximum(dot(far, enc_2) + bias_2, 0.0)
    far_part = dot((far_act * far_act).astype(BF16), dec_2).astype(BF16)
    got_far = exchange(far_part, True)
    rectified = paired(odd, near_act, far_act, LINE)
    latent = (rectified * rectified).astype(BF16)
    summed = paired(odd, added(got_near), added(got_far), 1).astype(BF16)
    misfit = (added(exchange(summed, False)) + b_dec).astype(BF16)
    misfit_all = spread(spread(misfit, False), True)

    own = w_dec.shape[0]
    dec_out = contract_first(latent[:, own:], misfit_all).astype(BF16)
    dec_sent = other_core(dec_out)
    misfit_all, dec_out = lax.optimization_barrier((misfit_all, dec_out))
    slope = (contract_last(misfit_all, dec_2) * 2.0 * rectified).astype(BF16)
    slope = slope.reshape(LINE, 2, -1, slope.shape[1])
    near_slope = jnp.where(odd, slope[:, 1], slope[:, 0]).reshape(rows, -1)
    far_slope = jnp.where(odd, slope[:, 0], slope[:, 1]).reshape(rows, -1)
    slope = jnp.concatenate([near_slope, far_slope], axis=0)
    normal_in = jnp.concatenate([near, far], axis=0)
    enc_out = contract_first(normal_in, slope[:, own:]).astype(BF16)
    enc_sent = other_core(enc_out)
    latent, slope, enc_out = lax.optimization_barrier((latent, slope, enc_out))
    dec_sum = (contract_first(latent[:, :own], misfit_all) + dec_sent.astype(F32)) * factor
    enc_sum = (contract_first(normal_in, slope[:, :own]) + enc_sent.astype(F32)) * factor
    return enc_sum, dec_sum


def solution(mesh):
    fine = Mesh(mesh.devices.reshape(2, 2, 2, 4, 4), ("xl", "c", "xh", "z", "y"))
    return jax.shard_map(
        on_device,
        mesh=fine,
        in_specs=(
            P(ROWS, None),
            P(),
            P(None, HIDDEN),
            P(None, HIDDEN),
            P(HIDDEN, None),
            P(None, ROWS + HIDDEN),
            P(ROWS + HIDDEN),
            P(ROWS + HIDDEN, None),
            P(),
        ),
        out_specs=(P(None, ROWS + HIDDEN), P(ROWS + HIDDEN, None)),
        check_vma=False,
    )
```

```python
import math

import jax
import jax.numpy as jnp
from jax import lax
from jax.sharding import Mesh
from jax.sharding import PartitionSpec as P


F32 = jnp.float32
BF16 = jnp.bfloat16
ROWS = ("xl", "c")
HIDDEN = ("xh", "z", "y")
ALL = ("xl", "c", "xh", "z", "y")


def scale_of(values):
    values = values.astype(F32)
    return lax.rsqrt(jnp.mean(values * values, axis=-1, keepdims=True) + 1e-06)


def normed(values, scale, pre_gain):
    return (values.astype(F32) * scale * (1.0 + pre_gain)).astype(BF16)


def dot(left, right):
    return jnp.dot(left, right, preferred_element_type=F32)


def contract_first(left, right):
    return lax.dot_general(left, right, (((0,), (0,)), ((), ())), preferred_element_type=F32)


def contract_last(left, right):
    return lax.dot_general(left, right, (((1,), (1,)), ((), ())), preferred_element_type=F32)


def index_of(x, core, z, y):
    return (((x % 2) * 2 + core) * 2 + x // 2) * 16 + z * 4 + y


def devices():
    return [(x, core, z, y) for x in range(4) for core in range(2) for z in range(4) for y in range(4)]


def far_rows(values):
    pairs = [
        (index_of(x, core, z, y), index_of((x + 1 - 2 * core) % 4, core, z, y))
        for x, core, z, y in devices()
    ]
    return lax.ppermute(values, ALL, pairs)


def groups_of_8(first):
    groups = {}
    for x, core, z, y in devices():
        line, across = (z, x) if core == 0 else (x, z)
        turned = (y + 1 - core) % 4
        group, place = (across, turned // 2), (line, min(turned, 3 - turned))
        key, order = (group, place) if first else (place, group)
        groups.setdefault((core, key), []).append((order, index_of(x, core, z, y)))
    return [[device for _, device in sorted(members)] for _, members in sorted(groups.items())]


def exchange(values, first):
    return lax.all_to_all(values, ALL, 0, 0, axis_index_groups=groups_of_8(first), tiled=True)


def other_core(values):
    return lax.ppermute(values, "c", [(0, 1), (1, 0)])


def added(blocks):
    total = blocks[0].astype(F32)
    for block in blocks[1:]:
        total = total + block.astype(F32)
    return total


def swap_if(flag, values):
    half = values.shape[0] // 2
    return jnp.where(flag, jnp.concatenate([values[half:], values[:half]], axis=0), values)


def on_device(resid_stream, pre_gain, w_gate, w_up, w_down, w_enc, b_enc, w_dec, b_dec):
    rows, width = resid_stream.shape
    factor = 1.0 / math.sqrt(rows * lax.axis_size(ROWS))
    odd = lax.axis_index("xl") == 1

    far_resid = far_rows(resid_stream)
    enc_2 = jnp.concatenate([w_enc, other_core(w_enc)], axis=1)
    dec_2 = jnp.concatenate([w_dec, other_core(w_dec)], axis=0)
    far_bias = other_core(b_enc)
    bias_2 = jnp.concatenate([b_enc, far_bias], axis=0).astype(F32)

    scale = scale_of(resid_stream)
    far_scale = far_rows(scale)
    near = normed(resid_stream, scale, pre_gain)
    hidden_units = (jax.nn.gelu(dot(near, w_gate), approximate=True) * dot(near, w_up)).astype(BF16)
    mine = swap_if(odd, jnp.concatenate([hidden_units, jnp.zeros_like(hidden_units)], axis=0))
    target = dot(mine, w_down)
    near_act = jnp.maximum(dot(near, enc_2) + bias_2, 0.0)
    far_resid, target, near_act, dec_2 = lax.optimization_barrier((far_resid, target, near_act, dec_2))
    far = normed(far_resid, far_scale, pre_gain)
    far_act = jnp.maximum(dot(far, enc_2) + bias_2, 0.0)
    rectified = swap_if(odd, jnp.concatenate([near_act, far_act], axis=0))
    latent = (rectified * rectified).astype(BF16)
    part = (dot(latent, dec_2) - target).astype(BF16)

    arrived = exchange(part.reshape(8, part.shape[0] // 8, width), True)
    summed = added(arrived).astype(BF16)
    arrived = exchange(summed.reshape(8, summed.shape[0] // 8, width), False)
    misfit = (added(arrived) + b_dec).astype(BF16)
    for first in (False, True):
        spread = jnp.broadcast_to(misfit[None], (8,) + misfit.shape)
        misfit = exchange(spread, first).reshape(8 * misfit.shape[0], width)
    misfit_all = misfit

    own = w_dec.shape[0]
    dec_out = contract_first(latent[:, own:], misfit_all).astype(BF16)
    dec_sent = other_core(dec_out)
    misfit_all, dec_out = lax.optimization_barrier((misfit_all, dec_out))
    slope = (contract_last(misfit_all, dec_2) * 2.0 * rectified).astype(BF16)
    slope = swap_if(odd, slope)
    normal_in = jnp.concatenate([near, far], axis=0)
    enc_out = contract_first(normal_in, slope[:, own:]).astype(BF16)
    enc_sent = other_core(enc_out)
    latent, slope, enc_out = lax.optimization_barrier((latent, slope, enc_out))
    dec_sum = (contract_first(latent[:, :own], misfit_all) + dec_sent.astype(F32)) * factor
    enc_sum = (contract_first(normal_in, slope[:, :own]) + enc_sent.astype(F32)) * factor
    return enc_sum, dec_sum


def solution(mesh):
    fine = Mesh(mesh.devices.reshape(2, 2, 2, 4, 4), ("xl", "c", "xh", "z", "y"))
    return jax.shard_map(
        on_device,
        mesh=fine,
        in_specs=(
            P(ROWS, None),
            P(),
            P(None, HIDDEN),
            P(None, HIDDEN),
            P(HIDDEN, None),
            P(None, ROWS + HIDDEN),
            P(ROWS + HIDDEN),
            P(ROWS + HIDDEN, None),
            P(),
        ),
        out_specs=(P(None, ROWS + HIDDEN), P(ROWS + HIDDEN, None)),
        check_vma=False,
    )
```

```python
import math

import jax
import jax.numpy as jnp
from jax import lax
from jax.sharding import Mesh
from jax.sharding import PartitionSpec as P


F32 = jnp.float32
BF16 = jnp.bfloat16
ROWS = ("xl", "c")
HIDDEN = ("xh", "z", "y")
ALL = ("xl", "c", "xh", "z", "y")


def scale_of(values):
    values = values.astype(F32)
    return lax.rsqrt(jnp.mean(values * values, axis=-1, keepdims=True) + 1e-06)


def normed(values, scale, pre_gain):
    return (values.astype(F32) * scale * (1.0 + pre_gain)).astype(BF16)


def dot(left, right):
    return jnp.dot(left, right, preferred_element_type=F32)


def contract_first(left, right):
    return lax.dot_general(left, right, (((0,), (0,)), ((), ())), preferred_element_type=F32)


def contract_last(left, right):
    return lax.dot_general(left, right, (((1,), (1,)), ((), ())), preferred_element_type=F32)


def index_of(x, core, z, y):
    return (((x % 2) * 2 + core) * 2 + x // 2) * 16 + z * 4 + y


def devices():
    return [(x, core, z, y) for x in range(4) for core in range(2) for z in range(4) for y in range(4)]


def far_rows(values):
    pairs = [
        (index_of(x, core, z, y), index_of((x + 1 - 2 * core) % 4, core, z, y))
        for x, core, z, y in devices()
    ]
    return lax.ppermute(values, ALL, pairs)


def groups_of_8(first):
    groups = {}
    for x, core, z, y in devices():
        line, across = (x, z) if core == 0 else (z, x)
        turned = (y + 1 - core) % 4
        group, place = (across, turned // 2), (line, min(turned, 3 - turned))
        key, order = (group, place) if first else (place, group)
        groups.setdefault((core, key), []).append((order, index_of(x, core, z, y)))
    return [[device for _, device in sorted(members)] for _, members in sorted(groups.items())]


def exchange(values, first):
    return lax.all_to_all(values, ALL, 0, 0, axis_index_groups=groups_of_8(first), tiled=True)


def other_core(values):
    return lax.ppermute(values, "c", [(0, 1), (1, 0)])


def added(blocks):
    total = blocks[0].astype(F32)
    for block in blocks[1:]:
        total = total + block.astype(F32)
    return total


def swap_if(flag, values):
    half = values.shape[0] // 2
    return jnp.where(flag, jnp.concatenate([values[half:], values[:half]], axis=0), values)


def on_device(resid_stream, pre_gain, w_gate, w_up, w_down, w_enc, b_enc, w_dec, b_dec):
    rows, width = resid_stream.shape
    factor = 1.0 / math.sqrt(rows * lax.axis_size(ROWS))
    odd = lax.axis_index("xl") == 1

    far_resid = far_rows(resid_stream)
    enc_2 = jnp.concatenate([w_enc, other_core(w_enc)], axis=1)
    dec_2 = jnp.concatenate([w_dec, other_core(w_dec)], axis=0)
    bias_2 = jnp.concatenate([b_enc, other_core(b_enc)], axis=0).astype(F32)

    scale = scale_of(resid_stream)
    far_scale = far_rows(scale)
    near = normed(resid_stream, scale, pre_gain)
    hidden_units = (jax.nn.gelu(dot(near, w_gate), approximate=True) * dot(near, w_up)).astype(BF16)
    mine = swap_if(odd, jnp.concatenate([hidden_units, jnp.zeros_like(hidden_units)], axis=0))
    target = dot(mine, w_down)
    near_act = jnp.maximum(dot(near, enc_2) + bias_2, 0.0)
    far_resid, target, near_act, dec_2 = lax.optimization_barrier((far_resid, target, near_act, dec_2))
    far = normed(far_resid, far_scale, pre_gain)
    far_act = jnp.maximum(dot(far, enc_2) + bias_2, 0.0)
    rectified = swap_if(odd, jnp.concatenate([near_act, far_act], axis=0))
    latent = (rectified * rectified).astype(BF16)
    part = (dot(latent, dec_2) - target).astype(BF16)

    arrived = exchange(part.reshape(8, part.shape[0] // 8, width), True)
    summed = added(arrived).astype(BF16)
    arrived = exchange(summed.reshape(8, summed.shape[0] // 8, width), False)
    misfit = (added(arrived) + b_dec).astype(BF16)
    for first in (False, True):
        spread = jnp.broadcast_to(misfit[None], (8,) + misfit.shape)
        misfit = exchange(spread, first).reshape(8 * misfit.shape[0], width)
    misfit_all = misfit

    own = w_dec.shape[0]
    dec_out = contract_first(latent[:, own:], misfit_all).astype(BF16)
    dec_sent = other_core(dec_out)
    misfit_all, dec_out = lax.optimization_barrier((misfit_all, dec_out))
    slope = (contract_last(misfit_all, dec_2) * 2.0 * rectified).astype(BF16)
    slope = swap_if(odd, slope)
    normal_in = jnp.concatenate([near, far], axis=0)
    enc_out = contract_first(normal_in, slope[:, own:]).astype(BF16)
    enc_sent = other_core(enc_out)
    latent, slope, enc_out = lax.optimization_barrier((latent, slope, enc_out))
    dec_sum = (contract_first(latent[:, :own], misfit_all) + dec_sent.astype(F32)) * factor
    enc_sum = (contract_first(normal_in, slope[:, :own]) + enc_sent.astype(F32)) * factor
    return enc_sum, dec_sum


def solution(mesh):
    fine = Mesh(mesh.devices.reshape(2, 2, 2, 4, 4), ("xl", "c", "xh", "z", "y"))
    return jax.shard_map(
        on_device,
        mesh=fine,
        in_specs=(
            P(ROWS, None),
            P(),
            P(None, HIDDEN),
            P(None, HIDDEN),
            P(HIDDEN, None),
            P(None, ROWS + HIDDEN),
            P(ROWS + HIDDEN),
            P(ROWS + HIDDEN, None),
            P(),
        ),
        out_specs=(P(None, ROWS + HIDDEN), P(ROWS + HIDDEN, None)),
        check_vma=False,
    )
```
